32 devices in a mesh: row: 8 (over y, x, core), col: 4 (over z).
Axes of the slice: x: 2, y: 2, z: 4, core: 2. Of those that a mesh axis runs over, the one named last changes fastest.
Arguments:
- earlier_blocks: bfloat16 [32, 8, 128, 128], P('row', 'col'), may hold values from -0.5 to 0.5
- later_blocks: bfloat16 [8, 32, 128, 128], P('row', 'col'), may hold values from -6 to 6
- earlier_pattern: int32 [32, 8], P('row', 'col'), may hold values from 0 to 1, as said below
- later_pattern: int32 [8, 32], P('row', 'col'), may hold values from 0 to 1, as said below
- triples: int32 [32, 32, 48], P('row', 'col'), may hold values from 0 to 7
Outputs:
- composed: float32 [32, 32, 128, 128], P('row', 'col')
The draws below stay inside these ranges and needn't reach their ends.
Inputs may be any that keep to these rules, and one draw needn't show every extreme that they name: `earlier_pattern`: in each aligned share of 4 x 2 entries held by one device, at most 4 entries are 1, and exactly 4 in some share. `later_pattern`: in each aligned share of 1 x 8 entries held by one device, at most 4 entries are 1, and exactly 4 in some share.
All inputs are finite; a program needn't handle non-finite values.
Results may differ from the reference program's by a relative error of at most 0.0003.
Values may be sent and summed in bfloat16 or wider, within the bound.
A program may use at most 256 MiB of HBM per device.

```python
import jax
import jax.numpy as jnp
from jax import lax

BLK = 128
ROWB_DEV = 4
COLB_DEV = 8
KB_DEV = 1
TK = 48
ROWS = 32
COLS = 32
KB = 8
KA_DEV = 2
N_ROW = 8
N_COL = 4


def draw_pattern(key, shard_rows, shard_cols, grid_rows, grid_cols):
    count_each = shard_rows * shard_cols
    capacity = max(1, count_each // 2)
    shards = grid_rows * grid_cols
    key_count, key_full, key_order = jax.random.split(key, 3)
    counts = jax.random.randint(key_count, (shards,), (capacity + 1) // 2, capacity + 1)
    chosen = jax.random.randint(key_full, (), 0, shards)
    counts = jnp.where(jnp.arange(shards) == chosen, capacity, counts)
    scores = jax.random.randint(key_order, (shards, count_each), 0, 1 << 20) * count_each + jnp.arange(count_each)[None, :]
    rank_order = jnp.argsort(jnp.argsort(scores, axis=1), axis=1)
    live_flags = (rank_order < counts[:, None]).astype(jnp.int32)
    arranged = live_flags.reshape(grid_rows, grid_cols, shard_rows, shard_cols).transpose(0, 2, 1, 3)
    return arranged.reshape(grid_rows * shard_rows, grid_cols * shard_cols)


def draw_earlier_pattern(key, part):
    return draw_pattern(jax.random.fold_in(key, 11), ROWB_DEV, KA_DEV, N_ROW, N_COL)


def draw_later_pattern(key, part):
    return draw_pattern(jax.random.fold_in(key, 23), KB_DEV, COLB_DEV, N_ROW, N_COL)


def with_ends(result, own_key, low, high):
    longest = result.shape.index(max(result.shape))
    spots = []
    for shift in (0, 1):
        where = [jax.random.randint(jax.random.fold_in(own_key, axis), (), 0, length) for axis, length in enumerate(result.shape)]
        where[longest] = (where[longest] + shift) % result.shape[longest]
        spots.append(tuple(where))
    return result.at[spots[0]].set(low).at[spots[1]].set(high)


def steps_of(own_key, extent, cuts, low, top_value):
    level = 1.0
    for dim, parts in cuts:
        steps = jax.random.uniform(jax.random.fold_in(jax.random.fold_in(own_key, 6), dim), (parts,), jnp.float32, low / len(cuts), top_value / len(cuts))
        level = level * jnp.repeat(jnp.exp(steps), extent[dim] // parts).reshape((-1,) + (1,) * (len(extent) - 1 - dim))
    return level


def normal_values(rng, extent, deviation, reach, cuts=(), held_as=jnp.bfloat16):
    level = steps_of(rng, extent, cuts, -0.22, 0.18) if cuts else 1.0
    values = jax.random.normal(rng, extent, jnp.float32) * deviation * level
    return jnp.minimum(jnp.maximum(values, -reach), reach).astype(held_as)


def setup_inputs(seed: int = 0) -> dict:
    streams_of = jax.random.split(jax.random.key(seed), 6)
    return {
        "earlier_blocks": normal_values(streams_of[0], (ROWS, KB, BLK, BLK), BLK ** -0.5, 0.5, ((0, 8), (1, 4))),
        "later_blocks": normal_values(streams_of[1], (KB, COLS, BLK, BLK), 1.0, 6.0, ((0, 8), (1, 4))),
        "earlier_pattern": draw_earlier_pattern(jax.random.fold_in(streams_of[5], 71), 0),
        "later_pattern": draw_later_pattern(jax.random.fold_in(streams_of[5], 71), 0),
        "triples": with_ends(jax.random.randint(streams_of[4], (ROWS, COLS, TK), 0, KB), jax.random.fold_in(streams_of[4], 1), 0, KB - 1).astype(jnp.int32),
    }


def reference(earlier_blocks, later_blocks, earlier_pattern, later_pattern, triples):
    earlier_live = earlier_blocks * earlier_pattern[:, :, None, None].astype(jnp.bfloat16)
    later_live = later_blocks * later_pattern[:, :, None, None].astype(jnp.bfloat16)
    col_numbers = jnp.arange(later_live.shape[1], dtype=jnp.int32)[:, None]

    def one_row(inputs):
        row_blocks, row_triples = inputs
        earlier_pick = row_blocks[row_triples].astype(jnp.float32)
        later_pick = later_live[row_triples, col_numbers].astype(jnp.float32)
        return jnp.einsum("jtab,jtbc->jac", earlier_pick, later_pick, precision=lax.Precision.HIGHEST)

    return lax.map(one_row, (earlier_live, triples))
```

```python
import functools

import jax
import jax.numpy as jnp
from jax import lax
from jax.experimental import pallas as pl
from jax.experimental.pallas import tpu as pltpu
from jax.sharding import PartitionSpec as P

MESH = pl.DeviceIdType.MESH
LANES = 128


def slot_positions(pattern_ref, capacity):
    count_a, count_b = pattern_ref.shape
    slots = []
    for slot in range(capacity):
        at_a, at_b, found = jnp.int32(0), jnp.int32(0), jnp.int32(0)
        rank = jnp.int32(0)
        for a in range(count_a):
            for b in range(count_b):
                live = pattern_ref[a, b]
                hit = jnp.logical_and(live == 1, rank == slot)
                at_a = jnp.where(hit, a, at_a)
                at_b = jnp.where(hit, b, at_b)
                found = jnp.where(hit, 1, found)
                rank = rank + live
        slots.append((at_a, at_b, found))
    return slots


def pack(blocks_ref, pattern_ref, packed_ref, meta_ref):
    lane = lax.broadcasted_iota(jnp.int32, meta_ref.shape, 1)
    meta = jnp.zeros(meta_ref.shape, jnp.int32)
    for slot, (at_a, at_b, found) in enumerate(slot_positions(pattern_ref, packed_ref.shape[0])):
        packed_ref[slot] = blocks_ref[at_a, at_b]
        for part, value in enumerate((at_a, at_b, found)):
            meta = jnp.where(lane == 3 * slot + part, value, meta)
    meta_ref[...] = meta


def gather_kernel(
    n_row, n_col, middle,
    e_ref, l_ref, ep_ref, lp_ref, t_ref,
    eg_ref, lg_ref, em_ref, lm_ref, cnt_ref,
    pe_ref, pl_ref, me_ref, ml_ref,
    send_e, recv_e, send_l, recv_l, send_f, recv_f, local_sem,
):
    row, col = lax.axis_index("row"), lax.axis_index("col")
    partner = row + 1 - 2 * lax.rem(row, 2)
    row_steps = range(1, n_row // 2)
    col_steps = range(1, n_col)
    row_to = [(lax.rem(row + 2 * d, n_row), col) for d in row_steps]
    col_to = [(row, lax.rem(col + d, n_col)) for d in col_steps]

    barrier = pltpu.get_barrier_semaphore()
    others = row_to + col_to + [(partner, col)]
    for other in others:
        pl.semaphore_signal(barrier, inc=1, device_id=other, device_id_type=MESH)
    pack(l_ref, lp_ref, pl_ref, ml_ref)
    pack(e_ref, ep_ref, pe_ref, me_ref)
    pl.semaphore_wait(barrier, len(others))

    def remote(src, dst, send, recv, device):
        return pltpu.make_async_remote_copy(
            src_ref=src, dst_ref=dst, send_sem=send, recv_sem=recv,
            device_id=device, device_id_type=MESH,
        )

    def pair(srcs, dsts, where, send, recv, d, device):
        return [
            remote(srcs[n], dsts[n].at[where], send.at[n, d], recv.at[n, d], device)
            for n in range(2)
        ]

    later_out, earlier_out = (lg_ref, lm_ref), (eg_ref, em_ref)
    later_own, earlier_own = (pl_ref, ml_ref), (pe_ref, me_ref)
    to_rows = [
        pair(later_own, later_out, row, send_l, recv_l, d, device)
        for d, device in zip(row_steps, row_to)
    ]
    to_cols = [
        pair(earlier_own, earlier_out, col, send_e, recv_e, d, device)
        for d, device in zip(col_steps, col_to)
    ]
    forwards = [pair(later_own, later_out, row, send_f, recv_f, 0, (partner, col))]
    for group in to_rows + to_cols + forwards:
        for copy in group:
            copy.start()
    locals_ = [
        pltpu.make_async_copy(src, dst, local_sem.at[n])
        for n, (src, dst) in enumerate((
            (pl_ref, lg_ref.at[row]), (ml_ref, lm_ref.at[row]),
            (pe_ref, eg_ref.at[col]), (me_ref, em_ref.at[col]),
        ))
    ]
    for copy in locals_:
        copy.start()

    rows, cols, listed = t_ref.shape
    lane = lax.broadcasted_iota(jnp.int32, (cols, LANES), 1)
    for i in range(rows):
        numbers = t_ref[i]
        counts = jnp.zeros((cols, LANES), jnp.float32)
        for k in range(middle):
            hits = jnp.sum(jnp.where(numbers == k, 1.0, 0.0), axis=1, keepdims=True)
            counts = jnp.where(lane == k, hits, counts)
        cnt_ref[pl.ds(i * cols, cols), :] = counts

    for d, group in zip(row_steps, to_rows):
        for copy in group:
            copy.wait_recv()
        source = lax.rem(row + n_row - 2 * d, n_row)
        onward = pair(
            (lg_ref.at[source], lm_ref.at[source]), later_out, source,
            send_f, recv_f, d, (partner, col),
        )
        for copy in onward:
            copy.start()
        forwards.append(onward)
    for group in to_cols + forwards:
        for copy in group:
            copy.wait_recv()
    for group in to_rows + to_cols + forwards:
        for copy in group:
            copy.wait_send()
    for copy in locals_:
        copy.wait()


def compose_kernel(early_ka, late_kb, eg_ref, lg_ref, em_ref, lm_ref, cnt_ref, out_ref):
    n_col, slots_e = eg_ref.shape[:2]
    slots_l = lg_ref.shape[1]
    rows, cols = out_ref.shape[:2]
    out_ref[...] = jnp.zeros_like(out_ref)
    for c in range(n_col):
        for s in range(slots_e):
            i = em_ref[c, 0, 3 * s]
            k = c * early_ka + em_ref[c, 0, 3 * s + 1]
            live_e = em_ref[c, 0, 3 * s + 2]
            source = k // late_kb if late_kb > 1 else k
            later = jnp.concatenate([lg_ref[source, u] for u in range(slots_l)], axis=1)
            product = jnp.dot(eg_ref[c, s], later, preferred_element_type=jnp.float32)
            for u in range(slots_l):
                k_l = source * late_kb + lm_ref[source, 0, 3 * u]
                j = lm_ref[source, 0, 3 * u + 1]
                live = jnp.logical_and(live_e * lm_ref[source, 0, 3 * u + 2] == 1, k_l == k)
                weight = jnp.where(live, cnt_ref[i * cols + j, k], 0.0)
                out_ref[i, j] += weight * product[:, u * LANES:(u + 1) * LANES]


def on_device(n_row, n_col, earlier_blocks, later_blocks, earlier_pattern, later_pattern, triples):
    rows, early_ka, side, _ = earlier_blocks.shape
    late_kb, cols = later_blocks.shape[:2]
    slots_e = max(1, rows * early_ka // 2)
    slots_l = max(1, late_kb * cols // 2)
    middle = n_row * late_kb
    vmem = pl.BlockSpec(memory_space=pltpu.VMEM)
    smem = pl.BlockSpec(memory_space=pltpu.SMEM)
    hbm = pl.BlockSpec(memory_space=pl.ANY)
    block = jnp.bfloat16
    eg, lg, em, lm, counts = pl.pallas_call(
        functools.partial(gather_kernel, n_row, n_col, middle),
        out_shape=(
            jax.ShapeDtypeStruct((n_col, slots_e, side, side), block),
            jax.ShapeDtypeStruct((n_row, slots_l, side, side), block),
            jax.ShapeDtypeStruct((n_col, 1, LANES), jnp.int32),
            jax.ShapeDtypeStruct((n_row, 1, LANES), jnp.int32),
            jax.ShapeDtypeStruct((rows * cols, LANES), jnp.float32),
        ),
        in_specs=[vmem, vmem, smem, smem, vmem],
        out_specs=(hbm, hbm, hbm, hbm, vmem),
        scratch_shapes=[
            pltpu.VMEM((slots_e, side, side), block),
            pltpu.VMEM((slots_l, side, side), block),
            pltpu.VMEM((1, LANES), jnp.int32),
            pltpu.VMEM((1, LANES), jnp.int32),
            pltpu.SemaphoreType.DMA((2, n_col)),
            pltpu.SemaphoreType.DMA((2, n_col)),
            pltpu.SemaphoreType.DMA((2, n_row)),
            pltpu.SemaphoreType.DMA((2, n_row)),
            pltpu.SemaphoreType.DMA((2, n_row)),
            pltpu.SemaphoreType.DMA((2, n_row)),
            pltpu.SemaphoreType.DMA((4,)),
        ],
        compiler_params=pltpu.CompilerParams(collective_id=0, has_side_effects=True),
        name="gather_live",
    )(earlier_blocks, later_blocks, earlier_pattern, later_pattern, triples)
    return pl.pallas_call(
        functools.partial(compose_kernel, early_ka, late_kb),
        out_shape=jax.ShapeDtypeStruct((rows, cols, side, side), jnp.float32),
        in_specs=[vmem, vmem, smem, smem, smem],
        out_specs=vmem,
        name="compose",
    )(eg, lg, em, lm, counts)


def solution(mesh):
    return jax.shard_map(
        functools.partial(on_device, mesh.shape["row"], mesh.shape["col"]),
        mesh=mesh,
        in_specs=(
            P("row", "col", None, None),
            P("row", "col", None, None),
            P("row", "col"),
            P("row", "col"),
            P("row", "col", None),
        ),
        out_specs=P("row", "col", None, None),
        check_vma=False,
    )
```

```python
import functools

import jax
import jax.numpy as jnp
from jax import lax
from jax.experimental import pallas as pl
from jax.experimental.pallas import tpu as pltpu
from jax.sharding import PartitionSpec as P

MESH = pl.DeviceIdType.MESH
LANES = 128


def slot_positions(pattern, count_a, count_b, capacity):
    slots = []
    for slot in range(capacity):
        at_a, at_b, found = jnp.int32(0), jnp.int32(0), jnp.int32(0)
        rank = jnp.int32(0)
        for a in range(count_a):
            for b in range(count_b):
                live = pattern(a, b)
                hit = jnp.logical_and(live == 1, rank == slot)
                at_a = jnp.where(hit, a, at_a)
                at_b = jnp.where(hit, b, at_b)
                found = jnp.where(hit, 1, found)
                rank = rank + live
        slots.append((at_a, at_b, found))
    return slots


def pack(blocks_ref, pattern, packed_ref, meta_ref):
    lane = lax.broadcasted_iota(jnp.int32, meta_ref.shape, 1)
    meta = jnp.zeros(meta_ref.shape, jnp.int32)
    slots = slot_positions(pattern, *blocks_ref.shape[:2], packed_ref.shape[0])
    for slot, (at_a, at_b, found) in enumerate(slots):
        packed_ref[slot] = blocks_ref[at_a, at_b]
        for part, value in enumerate((at_a, at_b, found)):
            meta = jnp.where(lane == 3 * slot + part, value, meta)
    meta_ref[...] = meta


def gather_kernel(
    n_row, n_col, middle,
    e_ref, l_ref, ep_ref, lp_ref, t_ref,
    eg_ref, lg_ref, em_ref, lm_ref, cnt_ref,
    pe_ref, pl_ref, me_ref, ml_ref,
    send_e, recv_e, send_l, recv_l, send_f, recv_f, local_sem,
):
    row, col = lax.axis_index("row"), lax.axis_index("col")
    partner = row + 1 - 2 * lax.rem(row, 2)
    row_steps = range(1, n_row // 2)
    row_to = [(lax.rem(row + 2 * d, n_row), col) for d in row_steps]
    slots_e = pe_ref.shape[0]
    has_right = col < n_col - 1
    has_left = col > 0

    barrier = pltpu.get_barrier_semaphore()
    others = row_to + [(partner, col)]
    for other in others:
        pl.semaphore_signal(barrier, inc=1, device_id=other, device_id_type=MESH)
    for there, step in ((has_right, 1), (has_left, -1)):
        @pl.when(there)
        def _():
            pl.semaphore_signal(
                barrier, inc=1, device_id=(row, col + step), device_id_type=MESH
            )
    pack(e_ref, lambda a, b: ep_ref[b, a], pe_ref, me_ref)
    pack(l_ref, lambda a, b: lp_ref[a, b], pl_ref, ml_ref)
    ends = has_right.astype(jnp.int32) + has_left.astype(jnp.int32)
    pl.semaphore_wait(barrier, len(others) + ends)

    def remote(src, dst, send, recv, device):
        return pltpu.make_async_remote_copy(
            src_ref=src, dst_ref=dst, send_sem=send, recv_sem=recv,
            device_id=device, device_id_type=MESH,
        )

    def pair(srcs, dsts, where, send, recv, d, device):
        return [
            remote(srcs[n], dsts[n].at[where], send.at[n, d], recv.at[n, d], device)
            for n in range(2)
        ]

    def along(way, hop, chunk):
        step = 1 - 2 * way
        source = col - step * hop
        if chunk == slots_e:
            src = me_ref if hop == 0 else em_ref.at[source]
            dst = em_ref.at[source]
        else:
            src = pe_ref.at[chunk] if hop == 0 else eg_ref.at[source, chunk]
            dst = eg_ref.at[source, chunk]
        return remote(
            src, dst, send_e.at[way, hop, chunk], recv_e.at[way, hop, chunk],
            (row, col + step),
        )

    def sends(way, hop):
        if way == 0:
            return jnp.logical_and(has_right, col >= hop)
        return jnp.logical_and(has_left, col + hop < n_col)

    def receives(way, hop):
        return col >= hop + 1 if way == 0 else col + hop + 1 < n_col

    hops = range(n_col - 1)
    chunks = range(slots_e + 1)
    for chunk in chunks:
        for way in range(2):
            @pl.when(sends(way, 0))
            def _():
                along(way, 0, chunk).start()

    later_out, later_own = (lg_ref, lm_ref), (pl_ref, ml_ref)
    to_rows = [
        pair(later_own, later_out, row, send_l, recv_l, d, device)
        for d, device in zip(row_steps, row_to)
    ]
    forwards = [pair(later_own, later_out, row, send_f, recv_f, 0, (partner, col))]
    for group in to_rows + forwards:
        for copy in group:
            copy.start()
    locals_ = [
        pltpu.make_async_copy(src, dst, local_sem.at[n])
        for n, (src, dst) in enumerate((
            (pl_ref, lg_ref.at[row]), (ml_ref, lm_ref.at[row]),
            (pe_ref, eg_ref.at[col]), (me_ref, em_ref.at[col]),
        ))
    ]
    for copy in locals_:
        copy.start()

    rows, cols, listed = t_ref.shape
    lane = lax.broadcasted_iota(jnp.int32, (cols, LANES), 1)
    for i in range(rows):
        numbers = t_ref[i]
        counts = jnp.zeros((cols, LANES), jnp.float32)
        for k in range(middle):
            hits = jnp.sum(jnp.where(numbers == k, 1.0, 0.0), axis=1, keepdims=True)
            counts = jnp.where(lane == k, hits, counts)
        cnt_ref[pl.ds(i * cols, cols), :] = counts

    def land(hop):
        for chunk in chunks:
            for way in range(2):
                @pl.when(receives(way, hop))
                def _():
                    along(way, hop, chunk).wait_recv()
                if hop + 1 < n_col - 1:
                    @pl.when(sends(way, hop + 1))
                    def _():
                        along(way, hop + 1, chunk).start()

    for hop in hops[:-1]:
        land(hop)
    for d, group in zip(row_steps, to_rows):
        for copy in group:
            copy.wait_recv()
        source = lax.rem(row + n_row - 2 * d, n_row)
        onward = pair(
            (lg_ref.at[source], lm_ref.at[source]), later_out, source,
            send_f, recv_f, d, (partner, col),
        )
        for copy in onward:
            copy.start()
        forwards.append(onward)
    for hop in hops[-1:]:
        land(hop)
    for group in forwards:
        for copy in group:
            copy.wait_recv()
    for group in to_rows + forwards:
        for copy in group:
            copy.wait_send()
    for hop in hops:
        for way in range(2):
            @pl.when(sends(way, hop))
            def _():
                for chunk in chunks:
                    along(way, hop, chunk).wait_send()
    for copy in locals_:
        copy.wait()


def compose_kernel(early_ka, late_kb, eg_ref, lg_ref, em_ref, lm_ref, cnt_ref, out_ref):
    n_col, slots_e = eg_ref.shape[:2]
    slots_l = lg_ref.shape[1]
    rows, cols = out_ref.shape[:2]
    out_ref[...] = jnp.zeros_like(out_ref)
    for c in range(n_col):
        for s in range(slots_e):
            i = em_ref[c, 0, 3 * s]
            k = c * early_ka + em_ref[c, 0, 3 * s + 1]
            live_e = em_ref[c, 0, 3 * s + 2]
            source = k // late_kb if late_kb > 1 else k
            later = jnp.concatenate([lg_ref[source, u] for u in range(slots_l)], axis=1)
            product = jnp.dot(eg_ref[c, s], later, preferred_element_type=jnp.float32)
            for u in range(slots_l):
                k_l = source * late_kb + lm_ref[source, 0, 3 * u]
                j = lm_ref[source, 0, 3 * u + 1]
                live = jnp.logical_and(live_e * lm_ref[source, 0, 3 * u + 2] == 1, k_l == k)
                weight = jnp.where(live, cnt_ref[i * cols + j, k], 0.0)
                out_ref[i, j] += weight * product[:, u * LANES:(u + 1) * LANES]


def on_device(n_row, n_col, earlier_blocks, later_blocks, earlier_pattern, later_pattern, triples):
    rows, early_ka, side, _ = earlier_blocks.shape
    late_kb, cols = later_blocks.shape[:2]
    slots_e = max(1, rows * early_ka // 2)
    slots_l = max(1, late_kb * cols // 2)
    middle = n_row * late_kb
    vmem = pl.BlockSpec(memory_space=pltpu.VMEM)
    smem = pl.BlockSpec(memory_space=pltpu.SMEM)
    hbm = pl.BlockSpec(memory_space=pl.ANY)
    block = jnp.bfloat16
    eg, lg, em, lm, counts = pl.pallas_call(
        functools.partial(gather_kernel, n_row, n_col, middle),
        out_shape=(
            jax.ShapeDtypeStruct((n_col, slots_e, side, side), block),
            jax.ShapeDtypeStruct((n_row, slots_l, side, side), block),
            jax.ShapeDtypeStruct((n_col, 1, LANES), jnp.int32),
            jax.ShapeDtypeStruct((n_row, 1, LANES), jnp.int32),
            jax.ShapeDtypeStruct((rows * cols, LANES), jnp.float32),
        ),
        in_specs=[vmem, vmem, smem, smem, vmem],
        out_specs=(hbm, hbm, hbm, hbm, vmem),
        scratch_shapes=[
            pltpu.VMEM((slots_e, side, side), block),
            pltpu.VMEM((slots_l, side, side), block),
            pltpu.VMEM((1, LANES), jnp.int32),
            pltpu.VMEM((1, LANES), jnp.int32),
            pltpu.SemaphoreType.DMA((2, n_col, slots_e + 1)),
            pltpu.SemaphoreType.DMA((2, n_col, slots_e + 1)),
            pltpu.SemaphoreType.DMA((2, n_row)),
            pltpu.SemaphoreType.DMA((2, n_row)),
            pltpu.SemaphoreType.DMA((2, n_row)),
            pltpu.SemaphoreType.DMA((2, n_row)),
            pltpu.SemaphoreType.DMA((4,)),
        ],
        compiler_params=pltpu.CompilerParams(collective_id=0, has_side_effects=True),
        name="gather_live",
    )(earlier_blocks, later_blocks, earlier_pattern.T, later_pattern, triples)
    return pl.pallas_call(
        functools.partial(compose_kernel, early_ka, late_kb),
        out_shape=jax.ShapeDtypeStruct((rows, cols, side, side), jnp.float32),
        in_specs=[vmem, vmem, smem, smem, smem],
        out_specs=vmem,
        name="compose",
    )(eg, lg, em, lm, counts)


def solution(mesh):
    return jax.shard_map(
        functools.partial(on_device, mesh.shape["row"], mesh.shape["col"]),
        mesh=mesh,
        in_specs=(
            P("row", "col", None, None),
            P("row", "col", None, None),
            P("row", "col"),
            P("row", "col"),
            P("row", "col", None),
        ),
        out_specs=P("row", "col", None, None),
        check_vma=False,
    )
```

```python
import functools

import jax
import jax.numpy as jnp
from jax import lax
from jax.experimental import pallas as pl
from jax.experimental.pallas import tpu as pltpu
from jax.sharding import PartitionSpec as P

MESH = pl.DeviceIdType.MESH
LANES = 128


def slot_positions(pattern, count_a, count_b, capacity):
    slots = []
    for slot in range(capacity):
        at_a, at_b, found = jnp.int32(0), jnp.int32(0), jnp.int32(0)
        rank = jnp.int32(0)
        for a in range(count_a):
            for b in range(count_b):
                live = pattern(a, b)
                hit = jnp.logical_and(live == 1, rank == slot)
                at_a = jnp.where(hit, a, at_a)
                at_b = jnp.where(hit, b, at_b)
                found = jnp.where(hit, 1, found)
                rank = rank + live
        slots.append((at_a, at_b, found))
    return slots


def pack(blocks_ref, pattern, packed_ref, meta_ref):
    lane = lax.broadcasted_iota(jnp.int32, meta_ref.shape, 1)
    meta = jnp.zeros(meta_ref.shape, jnp.int32)
    slots = slot_positions(pattern, *blocks_ref.shape[:2], packed_ref.shape[0])
    for slot, (at_a, at_b, found) in enumerate(slots):
        packed_ref[slot] = blocks_ref[at_a, at_b]
        for part, value in enumerate((at_a, at_b, found)):
            meta = jnp.where(lane == 3 * slot + part, value, meta)
    meta_ref[...] = meta


def gather_kernel(
    n_row, n_col, middle,
    e_hbm, l_hbm, ep_ref, lp_ref, t_ref,
    eg_ref, lg_ref, em_ref, lm_ref, cnt_ref,
    e_ref, l_ref, pe_ref, pl_ref, me_ref, ml_ref,
    send_e, recv_e, send_l, recv_l, send_f, recv_f, local_sem, fetch_sem,
):
    row, col = lax.axis_index("row"), lax.axis_index("col")
    partner = row + 1 - 2 * lax.rem(row, 2)
    row_steps = range(1, n_row // 2)
    row_to = [(lax.rem(row + 2 * d, n_row), col) for d in row_steps]
    slots_e = pe_ref.shape[0]
    has_right = col < n_col - 1
    has_left = col > 0

    barrier = pltpu.get_barrier_semaphore()
    others = row_to + [(partner, col)]
    for other in others:
        pl.semaphore_signal(barrier, inc=1, device_id=other, device_id_type=MESH)
    for there, step in ((has_right, 1), (has_left, -1)):
        @pl.when(there)
        def _():
            pl.semaphore_signal(
                barrier, inc=1, device_id=(row, col + step), device_id_type=MESH
            )
    fetch_e = pltpu.make_async_copy(e_hbm, e_ref, fetch_sem.at[0])
    fetch_l = pltpu.make_async_copy(l_hbm, l_ref, fetch_sem.at[1])
    fetch_e.start()
    fetch_l.start()
    fetch_e.wait()
    pack(e_ref, lambda a, b: ep_ref[b, a], pe_ref, me_ref)
    fetch_l.wait()
    pack(l_ref, lambda a, b: lp_ref[a, b], pl_ref, ml_ref)
    ends = has_right.astype(jnp.int32) + has_left.astype(jnp.int32)
    pl.semaphore_wait(barrier, len(others) + ends)

    def remote(src, dst, send, recv, device):
        return pltpu.make_async_remote_copy(
            src_ref=src, dst_ref=dst, send_sem=send, recv_sem=recv,
            device_id=device, device_id_type=MESH,
        )

    def pair(srcs, dsts, where, send, recv, d, device):
        return [
            remote(srcs[n], dsts[n].at[where], send.at[n, d], recv.at[n, d], device)
            for n in range(2)
        ]

    def along(way, hop, chunk):
        step = 1 - 2 * way
        source = col - step * hop
        if chunk == slots_e:
            src = me_ref if hop == 0 else em_ref.at[source]
            dst = em_ref.at[source]
        else:
            src = pe_ref.at[chunk] if hop == 0 else eg_ref.at[source, chunk]
            dst = eg_ref.at[source, chunk]
        return remote(
            src, dst, send_e.at[way, hop, chunk], recv_e.at[way, hop, chunk],
            (row, col + step),
        )

    def sends(way, hop):
        if way == 0:
            return jnp.logical_and(has_right, col >= hop)
        return jnp.logical_and(has_left, col + hop < n_col)

    def receives(way, hop):
        return col >= hop + 1 if way == 0 else col + hop + 1 < n_col

    hops = range(n_col - 1)
    chunks = range(slots_e + 1)
    for chunk in chunks:
        for way in range(2):
            @pl.when(sends(way, 0))
            def _():
                along(way, 0, chunk).start()

    later_out, later_own = (lg_ref, lm_ref), (pl_ref, ml_ref)
    to_rows = [
        pair(later_own, later_out, row, send_l, recv_l, d, device)
        for d, device in zip(row_steps, row_to)
    ]
    forwards = [pair(later_own, later_out, row, send_f, recv_f, 0, (partner, col))]
    for group in to_rows + forwards:
        for copy in group:
            copy.start()
    locals_ = [
        pltpu.make_async_copy(src, dst, local_sem.at[n])
        for n, (src, dst) in enumerate((
            (pl_ref, lg_ref.at[row]), (ml_ref, lm_ref.at[row]),
            (pe_ref, eg_ref.at[col]), (me_ref, em_ref.at[col]),
        ))
    ]
    for copy in locals_:
        copy.start()

    rows, cols, listed = t_ref.shape
    lane = lax.broadcasted_iota(jnp.int32, (cols, LANES), 1)
    for i in range(rows):
        numbers = t_ref[i]
        counts = jnp.zeros((cols, LANES), jnp.float32)
        for k in range(middle):
            hits = jnp.sum(jnp.where(numbers == k, 1.0, 0.0), axis=1, keepdims=True)
            counts = jnp.where(lane == k, hits, counts)
        cnt_ref[pl.ds(i * cols, cols), :] = counts

    def land(hop):
        for chunk in chunks:
            for way in range(2):
                @pl.when(receives(way, hop))
                def _():
                    along(way, hop, chunk).wait_recv()
                if hop + 1 < n_col - 1:
                    @pl.when(sends(way, hop + 1))
                    def _():
                        along(way, hop + 1, chunk).start()

    for hop in hops[:-1]:
        land(hop)
    for d, group in zip(row_steps, to_rows):
        for copy in group:
            copy.wait_recv()
        source = lax.rem(row + n_row - 2 * d, n_row)
        onward = pair(
            (lg_ref.at[source], lm_ref.at[source]), later_out, source,
            send_f, recv_f, d, (partner, col),
        )
        for copy in onward:
            copy.start()
        forwards.append(onward)
    for hop in hops[-1:]:
        land(hop)
    for group in forwards:
        for copy in group:
            copy.wait_recv()
    for group in to_rows + forwards:
        for copy in group:
            copy.wait_send()
    for hop in hops:
        for way in range(2):
            @pl.when(sends(way, hop))
            def _():
                for chunk in chunks:
                    along(way, hop, chunk).wait_send()
    for copy in locals_:
        copy.wait()


def compose_kernel(
    early_ka, late_kb,
    eg_hbm, lg_hbm, em_ref, lm_ref, cnt_ref, out_ref, eg_ref, lg_ref, fetch_sem,
):
    fetches = [
        pltpu.make_async_copy(lg_hbm, lg_ref, fetch_sem.at[0]),
        pltpu.make_async_copy(eg_hbm, eg_ref, fetch_sem.at[1]),
    ]
    for copy in fetches:
        copy.start()
    n_col, slots_e = eg_ref.shape[:2]
    slots_l = lg_ref.shape[1]
    rows, cols = out_ref.shape[:2]
    out_ref[...] = jnp.zeros_like(out_ref)
    for copy in fetches:
        copy.wait()
    for c in range(n_col):
        for s in range(slots_e):
            i = em_ref[c, 0, 3 * s]
            k = c * early_ka + em_ref[c, 0, 3 * s + 1]
            live_e = em_ref[c, 0, 3 * s + 2]
            source = k // late_kb if late_kb > 1 else k
            later = jnp.concatenate([lg_ref[source, u] for u in range(slots_l)], axis=1)
            product = jnp.dot(eg_ref[c, s], later, preferred_element_type=jnp.float32)
            for u in range(slots_l):
                k_l = source * late_kb + lm_ref[source, 0, 3 * u]
                j = lm_ref[source, 0, 3 * u + 1]
                live = jnp.logical_and(live_e * lm_ref[source, 0, 3 * u + 2] == 1, k_l == k)
                weight = jnp.where(live, cnt_ref[i * cols + j, k], 0.0)
                out_ref[i, j] += weight * product[:, u * LANES:(u + 1) * LANES]


def on_device(n_row, n_col, earlier_blocks, later_blocks, earlier_pattern, later_pattern, triples):
    rows, early_ka, side, _ = earlier_blocks.shape
    late_kb, cols = later_blocks.shape[:2]
    slots_e = max(1, rows * early_ka // 2)
    slots_l = max(1, late_kb * cols // 2)
    middle = n_row * late_kb
    vmem = pl.BlockSpec(memory_space=pltpu.VMEM)
    smem = pl.BlockSpec(memory_space=pltpu.SMEM)
    hbm = pl.BlockSpec(memory_space=pl.ANY)
    block = jnp.bfloat16
    eg, lg, em, lm, counts = pl.pallas_call(
        functools.partial(gather_kernel, n_row, n_col, middle),
        out_shape=(
            jax.ShapeDtypeStruct((n_col, slots_e, side, side), block),
            jax.ShapeDtypeStruct((n_row, slots_l, side, side), block),
            jax.ShapeDtypeStruct((n_col, 1, LANES), jnp.int32),
            jax.ShapeDtypeStruct((n_row, 1, LANES), jnp.int32),
            jax.ShapeDtypeStruct((rows * cols, LANES), jnp.float32),
        ),
        in_specs=[hbm, hbm, smem, smem, vmem],
        out_specs=(hbm, hbm, hbm, hbm, vmem),
        scratch_shapes=[
            pltpu.VMEM(earlier_blocks.shape, block),
            pltpu.VMEM(later_blocks.shape, block),
            pltpu.VMEM((slots_e, side, side), block),
            pltpu.VMEM((slots_l, side, side), block),
            pltpu.VMEM((1, LANES), jnp.int32),
            pltpu.VMEM((1, LANES), jnp.int32),
            pltpu.SemaphoreType.DMA((2, n_col, slots_e + 1)),
            pltpu.SemaphoreType.DMA((2, n_col, slots_e + 1)),
            pltpu.SemaphoreType.DMA((2, n_row)),
            pltpu.SemaphoreType.DMA((2, n_row)),
            pltpu.SemaphoreType.DMA((2, n_row)),
            pltpu.SemaphoreType.DMA((2, n_row)),
            pltpu.SemaphoreType.DMA((4,)),
            pltpu.SemaphoreType.DMA((2,)),
        ],
        compiler_params=pltpu.CompilerParams(collective_id=0, has_side_effects=True),
        name="gather_live",
    )(earlier_blocks, later_blocks, earlier_pattern.T, later_pattern, triples)
    return pl.pallas_call(
        functools.partial(compose_kernel, early_ka, late_kb),
        out_shape=jax.ShapeDtypeStruct((rows, cols, side, side), jnp.float32),
        in_specs=[hbm, hbm, smem, smem, smem],
        out_specs=vmem,
        scratch_shapes=[
            pltpu.VMEM(eg.shape, block),
            pltpu.VMEM(lg.shape, block),
            pltpu.SemaphoreType.DMA((2,)),
        ],
        name="compose",
    )(eg, lg, em, lm, counts)


def solution(mesh):
    return jax.shard_map(
        functools.partial(on_device, mesh.shape["row"], mesh.shape["col"]),
        mesh=mesh,
        in_specs=(
            P("row", "col", None, None),
            P("row", "col", None, None),
            P("row", "col"),
            P("row", "col"),
            P("row", "col", None),
        ),
        out_specs=P("row", "col", None, None),
        check_vma=False,
    )
```

```python
import functools

import jax
import jax.numpy as jnp
from jax import lax
from jax.experimental import pallas as pl
from jax.experimental.pallas import tpu as pltpu
from jax.sharding import PartitionSpec as P

MESH = pl.DeviceIdType.MESH
LANES = 128


def slot_positions(pattern, count_a, count_b, capacity):
    slots = []
    for slot in range(capacity):
        at_a, at_b, found = jnp.int32(0), jnp.int32(0), jnp.int32(0)
        rank = jnp.int32(0)
        for a in range(count_a):
            for b in range(count_b):
                live = pattern(a, b)
                hit = jnp.logical_and(live == 1, rank == slot)
                at_a = jnp.where(hit, a, at_a)
                at_b = jnp.where(hit, b, at_b)
                found = jnp.where(hit, 1, found)
                rank = rank + live
        slots.append((at_a, at_b, found))
    return slots


def pack(blocks_ref, pattern, packed_ref, meta_ref):
    lane = lax.broadcasted_iota(jnp.int32, meta_ref.shape, 1)
    meta = jnp.zeros(meta_ref.shape, jnp.int32)
    slots = slot_positions(pattern, *blocks_ref.shape[:2], packed_ref.shape[0])
    for slot, (at_a, at_b, found) in enumerate(slots):
        packed_ref[slot] = blocks_ref[at_a, at_b]
        for part, value in enumerate((at_a, at_b, found)):
            meta = jnp.where(lane == 3 * slot + part, value, meta)
    meta_ref[...] = meta


def gather_kernel(
    n_row, n_col, middle,
    e_hbm, l_hbm, ep_ref, lp_ref, t_ref,
    eg_ref, lg_ref, em_ref, lm_ref, cnt_ref,
    e_ref, l_ref, pe_ref, pl_ref, me_ref, ml_ref,
    send_e, recv_e, send_l, recv_l, send_f, recv_f, local_sem, fetch_sem,
):
    row, col = lax.axis_index("row"), lax.axis_index("col")
    partner = row + 1 - 2 * lax.rem(row, 2)
    row_steps = range(1, n_row // 2)
    row_to = [(lax.rem(row + 2 * d, n_row), col) for d in row_steps]
    slots_e = pe_ref.shape[0]
    has_right = col < n_col - 1
    has_left = col > 0

    barrier = pltpu.get_barrier_semaphore()
    others = row_to + [(partner, col)]
    for other in others:
        pl.semaphore_signal(barrier, inc=1, device_id=other, device_id_type=MESH)
    for there, step in ((has_right, 1), (has_left, -1)):
        @pl.when(there)
        def _():
            pl.semaphore_signal(
                barrier, inc=1, device_id=(row, col + step), device_id_type=MESH
            )
    fetch_e = pltpu.make_async_copy(e_hbm, e_ref, fetch_sem.at[0])
    fetch_l = pltpu.make_async_copy(l_hbm, l_ref, fetch_sem.at[1])
    fetch_e.start()
    fetch_l.start()
    fetch_e.wait()
    pack(e_ref, lambda a, b: ep_ref[b, a], pe_ref, me_ref)
    fetch_l.wait()
    pack(l_ref, lambda a, b: lp_ref[a, b], pl_ref, ml_ref)
    ends = has_right.astype(jnp.int32) + has_left.astype(jnp.int32)
    pl.semaphore_wait(barrier, len(others) + ends)

    def remote(src, dst, send, recv, device):
        return pltpu.make_async_remote_copy(
            src_ref=src, dst_ref=dst, send_sem=send, recv_sem=recv,
            device_id=device, device_id_type=MESH,
        )

    def pair(srcs, dsts, where, send, recv, d, device):
        return [
            remote(srcs[n], dsts[n].at[where], send.at[n, d], recv.at[n, d], device)
            for n in range(2)
        ]

    def along(way, hop, chunk):
        step = 1 - 2 * way
        source = col - step * hop
        if chunk == slots_e:
            src = me_ref if hop == 0 else em_ref.at[source]
            dst = em_ref.at[source]
        else:
            src = pe_ref.at[chunk] if hop == 0 else eg_ref.at[source, chunk]
            dst = eg_ref.at[source, chunk]
        return remote(
            src, dst, send_e.at[way, hop, chunk], recv_e.at[way, hop, chunk],
            (row, col + step),
        )

    def sends(way, hop):
        if way == 0:
            return jnp.logical_and(has_right, col >= hop)
        return jnp.logical_and(has_left, col + hop < n_col)

    def receives(way, hop):
        return col >= hop + 1 if way == 0 else col + hop + 1 < n_col

    hops = range(n_col - 1)
    chunks = range(slots_e + 1)
    for chunk in chunks:
        for way in range(2):
            @pl.when(sends(way, 0))
            def _():
                along(way, 0, chunk).start()

    later_out, later_own = (lg_ref, lm_ref), (pl_ref, ml_ref)
    to_rows = [
        pair(later_own, later_out, row, send_l, recv_l, d, device)
        for d, device in zip(row_steps, row_to)
    ]
    forwards = [pair(later_own, later_out, row, send_f, recv_f, 0, (partner, col))]
    for group in to_rows + forwards:
        for copy in group:
            copy.start()
    locals_ = [
        pltpu.make_async_copy(src, dst, local_sem.at[n])
        for n, (src, dst) in enumerate((
            (pl_ref, lg_ref.at[row]), (ml_ref, lm_ref.at[row]),
            (pe_ref, eg_ref.at[col]), (me_ref, em_ref.at[col]),
        ))
    ]
    for copy in locals_:
        copy.start()

    rows, cols, listed = t_ref.shape
    lane = lax.broadcasted_iota(jnp.int32, (cols, LANES), 1)
    for i in range(rows):
        numbers = t_ref[i]
        counts = jnp.zeros((cols, LANES), jnp.float32)
        for k in range(middle):
            hits = jnp.sum(jnp.where(numbers == k, 1.0, 0.0), axis=1, keepdims=True)
            counts = jnp.where(lane == k, hits, counts)
        cnt_ref[pl.ds(i * cols, cols), :] = counts

    def land(hop):
        for chunk in chunks:
            for way in range(2):
                @pl.when(receives(way, hop))
                def _():
                    along(way, hop, chunk).wait_recv()
                if hop + 1 < n_col - 1:
                    @pl.when(sends(way, hop + 1))
                    def _():
                        along(way, hop + 1, chunk).start()

    for hop in hops[:-1]:
        land(hop)
    for d, group in zip(row_steps, to_rows):
        for copy in group:
            copy.wait_recv()
        source = lax.rem(row + n_row - 2 * d, n_row)
        onward = pair(
            (lg_ref.at[source], lm_ref.at[source]), later_out, source,
            send_f, recv_f, d, (partner, col),
        )
        for copy in onward:
            copy.start()
        forwards.append(onward)
    for hop in hops[-1:]:
        land(hop)
    for group in forwards:
        for copy in group:
            copy.wait_recv()
    for group in to_rows + forwards:
        for copy in group:
            copy.wait_send()
    for hop in hops:
        for way in range(2):
            @pl.when(sends(way, hop))
            def _():
                for chunk in chunks:
                    along(way, hop, chunk).wait_send()
    for copy in locals_:
        copy.wait()


def compose_kernel(early_ka, late_kb, eg_ref, lg_ref, em_ref, lm_ref, cnt_ref, out_ref):
    n_col, slots_e = eg_ref.shape[:2]
    slots_l = lg_ref.shape[1]
    rows, cols = out_ref.shape[:2]
    out_ref[...] = jnp.zeros_like(out_ref)
    for c in range(n_col):
        for s in range(slots_e):
            i = em_ref[c, 0, 3 * s]
            k = c * early_ka + em_ref[c, 0, 3 * s + 1]
            live_e = em_ref[c, 0, 3 * s + 2]
            source = k // late_kb if late_kb > 1 else k
            later = jnp.concatenate([lg_ref[source, u] for u in range(slots_l)], axis=1)
            product = jnp.dot(eg_ref[c, s], later, preferred_element_type=jnp.float32)
            for u in range(slots_l):
                k_l = source * late_kb + lm_ref[source, 0, 3 * u]
                j = lm_ref[source, 0, 3 * u + 1]
                live = jnp.logical_and(live_e * lm_ref[source, 0, 3 * u + 2] == 1, k_l == k)
                weight = jnp.where(live, cnt_ref[i * cols + j, k], 0.0)
                out_ref[i, j] += weight * product[:, u * LANES:(u + 1) * LANES]


def on_device(n_row, n_col, earlier_blocks, later_blocks, earlier_pattern, later_pattern, triples):
    rows, early_ka, side, _ = earlier_blocks.shape
    late_kb, cols = later_blocks.shape[:2]
    slots_e = max(1, rows * early_ka // 2)
    slots_l = max(1, late_kb * cols // 2)
    middle = n_row * late_kb
    vmem = pl.BlockSpec(memory_space=pltpu.VMEM)
    smem = pl.BlockSpec(memory_space=pltpu.SMEM)
    hbm = pl.BlockSpec(memory_space=pl.ANY)
    block = jnp.bfloat16
    eg, lg, em, lm, counts = pl.pallas_call(
        functools.partial(gather_kernel, n_row, n_col, middle),
        out_shape=(
            jax.ShapeDtypeStruct((n_col, slots_e, side, side), block),
            jax.ShapeDtypeStruct((n_row, slots_l, side, side), block),
            jax.ShapeDtypeStruct((n_col, 1, LANES), jnp.int32),
            jax.ShapeDtypeStruct((n_row, 1, LANES), jnp.int32),
            jax.ShapeDtypeStruct((rows * cols, LANES), jnp.float32),
        ),
        in_specs=[hbm, hbm, smem, smem, vmem],
        out_specs=(hbm, hbm, hbm, hbm, vmem),
        scratch_shapes=[
            pltpu.VMEM(earlier_blocks.shape, block),
            pltpu.VMEM(later_blocks.shape, block),
            pltpu.VMEM((slots_e, side, side), block),
            pltpu.VMEM((slots_l, side, side), block),
            pltpu.VMEM((1, LANES), jnp.int32),
            pltpu.VMEM((1, LANES), jnp.int32),
            pltpu.SemaphoreType.DMA((2, n_col, slots_e + 1)),
            pltpu.SemaphoreType.DMA((2, n_col, slots_e + 1)),
            pltpu.SemaphoreType.DMA((2, n_row)),
            pltpu.SemaphoreType.DMA((2, n_row)),
            pltpu.SemaphoreType.DMA((2, n_row)),
            pltpu.SemaphoreType.DMA((2, n_row)),
            pltpu.SemaphoreType.DMA((4,)),
            pltpu.SemaphoreType.DMA((2,)),
        ],
        compiler_params=pltpu.CompilerParams(collective_id=0, has_side_effects=True),
        name="gather_live",
    )(earlier_blocks, later_blocks, earlier_pattern.T, later_pattern, triples)
    return pl.pallas_call(
        functools.partial(compose_kernel, early_ka, late_kb),
        out_shape=jax.ShapeDtypeStruct((rows, cols, side, side), jnp.float32),
        in_specs=[vmem, vmem, smem, smem, smem],
        out_specs=vmem,
        name="compose",
    )(eg, lg, em, lm, counts)


def solution(mesh):
    return jax.shard_map(
        functools.partial(on_device, mesh.shape["row"], mesh.shape["col"]),
        mesh=mesh,
        in_specs=(
            P("row", "col", None, None),
            P("row", "col", None, None),
            P("row", "col"),
            P("row", "col"),
            P("row", "col", None),
        ),
        out_specs=P("row", "col", None, None),
        check_vma=False,
    )
```
